32 devices in a mesh: row: 4 (over z), col: 8 (over y, x, core).
Axes of the slice: x: 2, y: 2, z: 4, core: 2. Of those that a mesh axis runs over, the one named last changes fastest.
Arguments:
- trail_adj: float32 [4, 3072, 12288], P(None, 'col', 'row'), as said below
- trail_factor: float32 [12288, 768], P(('row', 'col')), may hold values from -0.0546875 to 0.0546875
- trail_lbar: float32 [12288, 768], P(('row', 'col')), may hold values from -6 to 6
- head_factor: float32 [6, 65536], P(None, ('row', 'col')), as said below
- head_inverse: float32 [3, 65536], P(None, ('row', 'col')), as said below
- head_lbar: float32 [6, 65536], P(None, ('row', 'col')), may hold values from -6 to 6
Outputs:
- trail_cols: float32 [12288, 768], P(('row', 'col'))
- head_adj: float32 [6, 65536], P(None, ('row', 'col'))
The draws below stay inside these ranges and needn't reach their ends.
Inputs may be any that keep to these rules, and one draw needn't show every extreme that they name: trail_adj read as the matrix Z is exactly symmetric. The diagonal blocks F[k, k] of head_factor are lower triangular with a positive diagonal. Block k of head_inverse is lower triangular and is the inverse of F[k, k] up to float32 rounding.
All inputs are finite; a program needn't handle non-finite values.
Results may differ from the reference program's by a relative error of at most 0.00026.
Values sent between devices are 32-bit elements; how exact they have to be, the bound alone decides.
No kernel may reach another device: no remote copies, remote signals or barrier semaphores. Data moves between devices by JAX's collectives and lax.ppermute only.
A program may use at most 128 MiB of HBM per device.

```python
import math
import jax
import jax.numpy as jnp
from jax import lax

NB = 256
NT = 12288
N_ROW = 4


def head_pair(key):
    folded = jax.random.fold_in(key, 4051)
    subkeys = jax.random.split(folded, 3)
    diagonal = jax.random.uniform(subkeys[0], (3, NB), jnp.float32, 1.0, 2.0)
    strict_lower = jnp.tril(jax.random.normal(subkeys[1], (3, NB, NB), jnp.float32), -1) * (0.45 / math.sqrt(NB))
    diag_blocks = strict_lower + diagonal[:, :, None] * jnp.eye(NB, dtype=jnp.float32)[None, :, :]
    off_blocks = jax.random.normal(subkeys[2], (3, NB, NB), jnp.float32) / math.sqrt(NB)
    inverse = jnp.tril(jnp.linalg.inv(diag_blocks))
    factor = jnp.stack([diag_blocks[0], off_blocks[0], diag_blocks[1], off_blocks[1], off_blocks[2], diag_blocks[2]])
    return (factor.reshape(6, NB * NB), inverse.reshape(3, NB * NB))


def draw_head_factor(key, part):
    return head_pair(key)[0]


def draw_head_inverse(key, part):
    return head_pair(key)[1]


def draw_trail_adj(key, part):
    folded = jax.random.fold_in(key, 811)
    raw_values = jax.random.normal(folded, (NT, NT), jnp.float32)
    symmetric = (raw_values + raw_values.T) * 0.70710677
    return symmetric.reshape(N_ROW, NT // N_ROW, NT)


def block_levels(stream_key, dims, cuts, low, largest):
    level = 1.0
    for position, shards_of in cuts:
        heights = jax.random.uniform(jax.random.fold_in(jax.random.fold_in(stream_key, 6), position), (shards_of,), jnp.float32, low / len(cuts), largest / len(cuts))
        level = level * jnp.repeat(jnp.exp(heights), dims[position] // shards_of).reshape((-1,) + (1,) * (len(dims) - 1 - position))
    return level


def centred(own_key, extent, spread, limit, shards=(), held_as=jnp.bfloat16):
    drawn = spread * jax.random.normal(own_key, extent, jnp.float32)
    if shards:
        drawn = drawn * block_levels(own_key, extent, shards, -0.22, 0.18)
    return jnp.clip(drawn, -limit, limit).astype(held_as)


def setup_inputs(seed: int = 0) -> dict:
    splits = jax.random.split(jax.random.key(seed), 7)
    trail_adj = draw_trail_adj(jax.random.fold_in(splits[6], 71), 0)
    trail_factor = centred(splits[1], (NT, 3 * NB), NT ** -0.5, 0.0546875, ((0, 32),), jnp.float32)
    trail_lbar = centred(splits[2], (NT, 3 * NB), 1.0, 6.0, ((0, 32),), jnp.float32)
    head_factor = draw_head_factor(jax.random.fold_in(splits[6], 71), 0)
    head_inverse = draw_head_inverse(jax.random.fold_in(splits[6], 71), 0)
    head_lbar = centred(splits[5], (6, NB * NB), 1.0, 6.0, ((1, 32),), jnp.float32)
    return {"trail_adj": trail_adj, "trail_factor": trail_factor, "trail_lbar": trail_lbar, "head_factor": head_factor, "head_inverse": head_inverse, "head_lbar": head_lbar}


highest = lax.Precision.HIGHEST

def matmul(left, right):
    return jnp.dot(left.astype(jnp.float32), right.astype(jnp.float32), precision=highest, preferred_element_type=jnp.float32)

def contract_rows(left, right):
    return lax.dot_general(left.astype(jnp.float32), right.astype(jnp.float32), (((0,), (0,)), ((), ())), precision=highest, preferred_element_type=jnp.float32)

def pair_index(target, source):
    return target * (target + 1) // 2 + source

def halve_lower(matrix):
    return jnp.tril(matrix) - 0.5 * jnp.diag(jnp.diag(matrix))

def chol_adjoint(factor, inverse, totals):
    inner = halve_lower(matmul(factor.T, totals))
    mapped = matmul(matmul(inverse.T, inner), inverse)
    return 0.5 * (mapped + mapped.T)

def trail_column(column, product, lbar_rows, columns, factor_blocks, inverse_blocks, breadth):
    gradient = lbar_rows[:, column * breadth:(column + 1) * breadth] - 2.0 * product[:, column * breadth:(column + 1) * breadth]
    for source in range(column + 1, 3):
        gradient = gradient - 2.0 * matmul(columns[source], factor_blocks[pair_index(source, column)])
    return 0.5 * matmul(gradient, inverse_blocks[column])

def trail_terms_of(column, columns, factor_rows, breadth):
    own_rows = factor_rows[:, column * breadth:(column + 1) * breadth]
    terms = [contract_rows(2.0 * columns[column], own_rows)]
    for target in range(column + 1, 3):
        terms.append(contract_rows(columns[target], own_rows))
    return terms

def head_step(column, blocks, factor_blocks, inverse_blocks, lbar_blocks, sums):
    totals = lbar_blocks[pair_index(column, column)] - sums[0]
    for target in range(column + 1, 3):
        summed = sums[target - column]
        for source in range(column + 1, 3):
            if target >= source:
                mirror = blocks[pair_index(target, source)]
            else:
                mirror = blocks[pair_index(source, target)].T
            summed = summed + matmul(mirror, factor_blocks[pair_index(source, column)])
        carried = matmul(lbar_blocks[pair_index(target, column)] - 2.0 * summed, inverse_blocks[column])
        blocks[pair_index(target, column)] = 0.5 * carried
        totals = totals - contract_rows(carried, factor_blocks[pair_index(target, column)])
    blocks[pair_index(column, column)] = chol_adjoint(factor_blocks[pair_index(column, column)], inverse_blocks[column], totals)

def reference(trail_adj, trail_factor, trail_lbar, head_factor, head_inverse, head_lbar):
    adjoint = trail_adj.reshape(NT, NT)
    product = matmul(adjoint, trail_factor)
    factor_blocks = head_factor.reshape(6, NB, NB)
    inverse_blocks = head_inverse.reshape(3, NB, NB)
    lbar_blocks = head_lbar.reshape(6, NB, NB)
    columns = [None, None, None]
    for column in (2, 1, 0):
        columns[column] = trail_column(column, product, trail_lbar, columns, factor_blocks, inverse_blocks, NB)
    blocks = [None, None, None, None, None, None]
    for column in (2, 1, 0):
        sums = jnp.stack(trail_terms_of(column, columns, trail_factor, NB))
        head_step(column, blocks, factor_blocks, inverse_blocks, lbar_blocks, sums)
    return (jnp.concatenate(columns, axis=1), jnp.stack(blocks).reshape(6, NB * NB))
```

```python
import functools

import jax
import jax.numpy as jnp
from jax import lax
from jax.experimental import pallas as pl
from jax.experimental.pallas import tpu as pltpu
from jax.sharding import PartitionSpec as P


NB = 256


highest = lax.Precision.HIGHEST


def matmul(left, right):
    return jnp.dot(left, right, precision=highest, preferred_element_type=jnp.float32)


def contract_rows(left, right):
    return lax.dot_general(
        left, right, (((0,), (0,)), ((), ())), precision=highest, preferred_element_type=jnp.float32
    )


def pair_index(target, source):
    return target * (target + 1) // 2 + source


def halve_lower(matrix):
    return jnp.tril(matrix) - 0.5 * jnp.diag(jnp.diag(matrix))


def chol_adjoint(factor, inverse, totals):
    inner = halve_lower(matmul(factor.T, totals))
    mapped = matmul(matmul(inverse.T, inner), inverse)
    return 0.5 * (mapped + mapped.T)


def trail_column(column, product, lbar_rows, columns, factor_blocks, inverse_blocks, breadth):
    gradient = (
        lbar_rows[:, column * breadth : (column + 1) * breadth]
        - 2.0 * product[:, column * breadth : (column + 1) * breadth]
    )
    for source in range(column + 1, 3):
        gradient = gradient - 2.0 * matmul(
            columns[source], factor_blocks[pair_index(source, column)]
        )
    return 0.5 * matmul(gradient, inverse_blocks[column])


def trail_terms_of(column, columns, factor_rows, breadth):
    own_rows = factor_rows[:, column * breadth : (column + 1) * breadth]
    terms = [contract_rows(2.0 * columns[column], own_rows)]
    for target in range(column + 1, 3):
        terms.append(contract_rows(columns[target], own_rows))
    return terms


def head_step(column, blocks, factor_blocks, inverse_blocks, lbar_blocks, sums):
    totals = lbar_blocks[pair_index(column, column)] - sums[0]
    for target in range(column + 1, 3):
        summed = sums[target - column]
        for source in range(column + 1, 3):
            if target >= source:
                mirror = blocks[pair_index(target, source)]
            else:
                mirror = blocks[pair_index(source, target)].T
            summed = summed + matmul(mirror, factor_blocks[pair_index(source, column)])
        carried = matmul(
            lbar_blocks[pair_index(target, column)] - 2.0 * summed, inverse_blocks[column]
        )
        blocks[pair_index(target, column)] = 0.5 * carried
        totals = totals - contract_rows(carried, factor_blocks[pair_index(target, column)])
    blocks[pair_index(column, column)] = chol_adjoint(
        factor_blocks[pair_index(column, column)], inverse_blocks[column], totals
    )


def general_body(trail_adj, trail_factor, trail_lbar, head_factor, head_inverse, head_lbar):
    gathered = (
        lax.all_gather(head_factor, ("row", "col"), axis=1, tiled=True),
        lax.all_gather(head_inverse, ("row", "col"), axis=1, tiled=True),
        lax.all_gather(head_lbar, ("row", "col"), axis=1, tiled=True),
    )
    factor_blocks = gathered[0].reshape(6, NB, NB)
    inverse_blocks = gathered[1].reshape(3, NB, NB)
    lbar_blocks = gathered[2].reshape(6, NB, NB)
    adjoint_rows = trail_adj.reshape(-1, trail_adj.shape[2])
    factor_rows = lax.all_gather(trail_factor, "row", axis=0, tiled=True)
    product = lax.psum_scatter(
        contract_rows(adjoint_rows, factor_rows), "col", scatter_dimension=0, tiled=True
    )
    columns = [None, None, None]
    blocks = [None, None, None, None, None, None]
    for column in (2, 1, 0):
        columns[column] = trail_column(
            column, product, trail_lbar, columns, factor_blocks, inverse_blocks, NB
        )
        stacked = jnp.stack(trail_terms_of(column, columns, trail_factor, NB))
        sums = lax.psum(stacked, ("row", "col"))
        head_step(column, blocks, factor_blocks, inverse_blocks, lbar_blocks, sums)
    flattened = jnp.stack(blocks).reshape(6, NB * NB)
    share = flattened.shape[1] // (lax.axis_size("row") * lax.axis_size("col"))
    head_adj = lax.dynamic_slice_in_dim(flattened, lax.axis_index(("row", "col")) * share, share, 1)
    trail_cols = jnp.concatenate(columns, axis=1)
    return (trail_cols, head_adj)


F32, BF16 = jnp.float32, jnp.bfloat16
CORE, X, Y = 1, 2, 4
AXES = ("row", "col")


def split_bf16(value):
    high = value.astype(BF16)
    return high, (value - high.astype(F32)).astype(BF16)


def dot_bf16(left, right, dims=(1, 0)):
    return lax.dot_general(
        left, right, (((dims[0],), (dims[1],)), ((), ())), preferred_element_type=F32
    )


def dot3(left, right, dims=(1, 0)):
    left_high, left_low = split_bf16(left)
    right_high, right_low = split_bf16(right)
    return (
        dot_bf16(left_high, right_high, dims)
        + dot_bf16(left_high, right_low, dims)
        + dot_bf16(left_low, right_high, dims)
    )


def exchange(value, rows, cols, row_bits=0, col_bits=0):
    pairs = [
        (r * cols + c, (r ^ row_bits) * cols + (c ^ col_bits))
        for r in range(rows)
        for c in range(cols)
    ]
    return lax.ppermute(value, AXES, pairs)


def row_form_kernel(places, place_ref, z_ref, *refs):
    pieces, (out_ref, factor_ref) = refs[: len(places)], refs[len(places) :]
    width = out_ref.shape[-1]
    depth = pieces[0].shape[0]

    @pl.when(pl.program_id(0) == 0)
    def _():
        for piece, (rel, offset) in zip(pieces, places):
            start = pl.multiple_of((place_ref[1] ^ rel) * depth + offset, 128)
            high, low = split_bf16(piece[...])
            factor_ref[pl.ds(start, piece.shape[0]), :width] = high
            factor_ref[pl.ds(start, piece.shape[0]), width:] = low

    high, low = split_bf16(z_ref[0])
    both = dot_bf16(high, factor_ref[...])
    cross = dot_bf16(low, factor_ref[:, :width])
    out_ref[0] = both[:, :width] + both[:, width:] + cross


def row_form(trail_adj, places, pieces, place, order):
    rows, m, n = trail_adj.shape
    width = pieces[0].shape[1]
    count = len(order)

    def rel_of(step):
        rel = order[-1]
        for position in range(count - 1):
            rel = jnp.where(step == position, order[position], rel)
        return rel

    grid_spec = pltpu.PrefetchScalarGridSpec(
        num_scalar_prefetch=1,
        grid=(count,),
        in_specs=[pl.BlockSpec((1, m, n), lambda i, p: (p[0] ^ rel_of(i), 0, 0))]
        + [pl.BlockSpec(memory_space=pltpu.VMEM)] * len(pieces),
        out_specs=pl.BlockSpec((1, m, width), lambda i, p: (i, 0, 0)),
        scratch_shapes=[pltpu.VMEM((n, 2 * width), BF16)],
    )
    return pl.pallas_call(
        functools.partial(row_form_kernel, places),
        out_shape=jax.ShapeDtypeStruct((count, m, width), F32),
        grid_spec=grid_spec,
        compiler_params=pltpu.CompilerParams(vmem_limit_bytes=56 << 20),
        cost_estimate=pl.CostEstimate(
            flops=6 * count * m * n * width,
            bytes_accessed=4 * count * m * (n + width) + 4 * n * width,
            transcendentals=0,
        ),
        name="row_form",
    )(place, trail_adj, *pieces)


def col_form_kernel(rows, place_ref, *refs):
    z_refs, pieces = refs[:rows], refs[rows : 2 * rows]
    keep_ref, send_ref, factor_ref = refs[2 * rows :]
    m, width = pieces[0].shape

    @pl.when(pl.program_id(0) == 0)
    def _():
        for rel in range(rows):
            high, low = split_bf16(pieces[rel][...].T)
            factor_ref[:width, rel * m : (rel + 1) * m] = high
            factor_ref[width:, rel * m : (rel + 1) * m] = low

    z = jnp.concatenate([z_ref[0] for z_ref in z_refs], axis=0)
    high, low = split_bf16(z)
    both = dot_bf16(factor_ref[...], high)
    total = both[:width] + both[width:] + dot_bf16(factor_ref[:width, :], low)
    first = (place_ref[1] & CORE) == 0
    keep_ref[0] = jnp.where(first, total[:, :m], total[:, m:])
    send_ref[0] = jnp.where(first, total[:, m:], total[:, :m])


def col_form(trail_adj, pieces, place, order):
    rows, m, n = trail_adj.shape
    width = pieces[0].shape[1]
    count = len(order)

    def rel_of(step):
        rel = order[-1] // 2
        for position in range(count - 1):
            rel = jnp.where(step == position, order[position] // 2, rel)
        return rel

    def z_spec(rel_row):
        return pl.BlockSpec(
            (1, m, 2 * m), lambda i, p: (p[0] ^ rel_row, 0, (p[1] >> 1) ^ rel_of(i))
        )

    out = jax.ShapeDtypeStruct((count, width, m), F32)
    grid_spec = pltpu.PrefetchScalarGridSpec(
        num_scalar_prefetch=1,
        grid=(count,),
        in_specs=[z_spec(rel) for rel in range(rows)]
        + [pl.BlockSpec(memory_space=pltpu.VMEM)] * rows,
        out_specs=[pl.BlockSpec((1, width, m), lambda i, p: (i, 0, 0))] * 2,
        scratch_shapes=[pltpu.VMEM((2 * width, rows * m), BF16)],
    )
    return pl.pallas_call(
        functools.partial(col_form_kernel, rows),
        out_shape=[out, out],
        grid_spec=grid_spec,
        compiler_params=pltpu.CompilerParams(vmem_limit_bytes=56 << 20),
        cost_estimate=pl.CostEstimate(
            flops=6 * count * rows * m * 2 * m * width,
            bytes_accessed=4 * count * 2 * m * (rows * m + width) + 4 * rows * m * width,
            transcendentals=0,
        ),
        name="col_form",
    )(place, *[trail_adj] * rows, *pieces)


def tail_kernel(rels, n_alpha, n_beta, place_ref, *refs):
    alpha_refs, beta_refs = refs[:n_alpha], refs[n_alpha : n_alpha + n_beta]
    lbar_ref, own_ref, heads_ref, head_lbar_ref = refs[n_alpha + n_beta : n_alpha + n_beta + 4]
    cols_ref, keep_ref, send_ref, head_ref, blocks_ref = refs[n_alpha + n_beta + 4 :]
    devices = len(rels)
    step = NB // devices
    index = place_ref[2]

    def rows_of(rel):
        return pl.ds(pl.multiple_of((index ^ rel) * step, step), step)

    for position, rel in enumerate(rels):
        head_ref[:, rows_of(rel), :] = heads_ref[position]
    blocks_ref[...] = jnp.zeros_like(blocks_ref)
    blocks_ref[:, rows_of(0), :] = head_lbar_ref[...]

    def factor(target, source):
        return head_ref[pair_index(target, source)]

    def inverse(column):
        return head_ref[6 + column]

    def panel(value, column):
        return value[:, column * NB : (column + 1) * NB]

    alpha = sum(ref[...] for ref in alpha_refs[1:]) + alpha_refs[0][...]
    beta = sum(ref[...] for ref in beta_refs[1:]) + beta_refs[0][...]
    product = jnp.concatenate([alpha, beta.T], axis=1)
    gradient = 0.5 * lbar_ref[...] - product
    columns = [None, None, None]
    for column in (2, 1, 0):
        part = panel(gradient, column)
        for source in range(column + 1, 3):
            part = part - dot3(columns[source], factor(source, column))
        columns[column] = dot3(part, inverse(column))
        cols_ref[:, column * NB : (column + 1) * NB] = columns[column]

    blocks = [None] * 6
    line = lax.broadcasted_iota(jnp.int32, (NB, NB), 0)
    lane = lax.broadcasted_iota(jnp.int32, (NB, NB), 1)
    weight = jnp.where(line > lane, 1.0, jnp.where(line == lane, 0.5, 0.0))
    for column in (2, 1, 0):
        own = own_ref[:, column * NB : (column + 1) * NB]
        totals = blocks_ref[pair_index(column, column)] - dot3(2.0 * columns[column], own, (0, 0))
        for target in range(column + 1, 3):
            summed = dot3(columns[target], own, (0, 0))
            for source in range(column + 1, 3):
                if target >= source:
                    mirror = blocks[pair_index(target, source)]
                else:
                    mirror = blocks[pair_index(source, target)].T
                summed = summed + dot3(mirror, factor(source, column))
            carried = dot3(
                blocks_ref[pair_index(target, column)] - 2.0 * summed, inverse(column)
            )
            blocks[pair_index(target, column)] = 0.5 * carried
            totals = totals - dot3(carried, factor(target, column), (0, 0))
        inner = dot3(factor(column, column), totals, (0, 0)) * weight
        mapped = dot3(dot3(inverse(column), inner, (0, 0)), inverse(column))
        blocks[pair_index(column, column)] = 0.5 * (mapped + mapped.T)

    for pair in range(6):
        blocks_ref[pair] = blocks[pair]
    half = devices // 2
    for position, rel in enumerate(rels):
        out_ref = keep_ref if position < half else send_ref
        out_ref[position % half] = blocks_ref[:, rows_of(rel), :]


def tail(alphas, betas, trail_lbar, trail_factor, heads, head_lbar, place, rels):
    m, width = trail_lbar.shape
    devices, _, step, _ = heads.shape
    half = jax.ShapeDtypeStruct((devices // 2, 6, step, NB), F32)
    operands = [*alphas, *betas, trail_lbar, trail_factor, heads, head_lbar]
    return pl.pallas_call(
        functools.partial(tail_kernel, rels, len(alphas), len(betas)),
        out_shape=[jax.ShapeDtypeStruct((m, width), F32), half, half],
        in_specs=[pl.BlockSpec(memory_space=pltpu.SMEM)]
        + [pl.BlockSpec(memory_space=pltpu.VMEM)] * len(operands),
        out_specs=[pl.BlockSpec(memory_space=pltpu.VMEM)] * 3,
        scratch_shapes=[pltpu.VMEM((9, NB, NB), F32), pltpu.VMEM((6, NB, NB), F32)],
        compiler_params=pltpu.CompilerParams(vmem_limit_bytes=56 << 20),
        cost_estimate=pl.CostEstimate(
            flops=6 * NB * NB * (12 * m + 20 * NB),
            bytes_accessed=4 * (4 * m * width + 21 * NB * NB),
            transcendentals=0,
        ),
        name="tail",
    )(place, *operands)


def plane_sum(own, x_part, y_part, diagonal, swap, cut):
    first, second = cut(diagonal)
    via_x, via_y = swap(first, X), swap(second, Y)
    y_first, y_second = cut(y_part)
    x_first, x_second = cut(x_part)
    y_sum = jnp.concatenate([y_first + via_x, y_second], axis=0)
    x_sum = jnp.concatenate([x_first, x_second + via_y], axis=0)
    return own, swap(x_sum, X), swap(y_sum, Y)


def halves(value):
    middle = value.shape[0] // 2
    return value[:middle], value[middle:]


def fast_body(trail_adj, trail_factor, trail_lbar, head_factor, head_inverse, head_lbar):
    rows, cols = lax.axis_size("row"), lax.axis_size("col")
    row, col = lax.axis_index("row"), lax.axis_index("col")
    place = jnp.stack([row, col, row * cols + col]).astype(jnp.int32)
    m, width = trail_factor.shape
    swap = functools.partial(exchange, rows=rows, cols=cols)

    def swap_row(value, bits):
        return swap(value, row_bits=bits)

    def swap_col(value, bits):
        return swap(value, col_bits=bits)

    alpha_own, beta_own = trail_factor[:, : width // 2], trail_factor[:, width // 2 :]
    beta_rel = {0: beta_own}
    beta_rel[2] = swap_row(beta_own, 2)
    from_x, from_y = swap_col(alpha_own, X), swap_col(alpha_own, Y)
    beta_rel[1] = swap_row(beta_own, 1)
    middle = m // 2
    diagonal = (swap_col(from_y[:middle], X), swap_col(from_x[middle:], Y))
    pieces = [
        (alpha_own, 0, 0),
        (from_x, X, 0),
        (from_y, Y, 0),
        (diagonal[0], X | Y, 0),
        (diagonal[1], X | Y, middle),
    ]
    pieces += [(swap_col(value, CORE), rel | CORE, offset) for value, rel, offset in pieces]
    beta_rel[3] = swap_row(beta_rel[2], 1)

    heads = jnp.concatenate([head_factor, head_inverse], axis=0)
    step = heads.shape[1] // NB
    heads = heads.reshape(1, 9, step, NB)
    rels = [0]
    for row_bits, col_bits in ((2, 0), (1, 0), (0, X), (0, Y), (0, CORE)):
        heads = jnp.concatenate([heads, swap(heads, row_bits=row_bits, col_bits=col_bits)], axis=0)
        rels += [rel ^ (row_bits * cols + col_bits) for rel in rels]

    row_order = (3, 1, 2, 0)
    parts = row_form(
        trail_adj, [piece[1:] for piece in pieces], [piece[0] for piece in pieces], place, row_order
    )
    part = {rel: parts[position] for position, rel in enumerate(row_order)}
    far = part[2] + swap_row(part[3], 1)
    alphas = [part[0], swap_row(part[1], 1), swap_row(far, 2)]

    col_order = (X | Y, X, Y, 0)
    keep, send = col_form(trail_adj, [beta_rel[rel] for rel in range(rows)], place, col_order)
    sums = {
        rel: keep[position] + swap_col(send[position], CORE)
        for position, rel in enumerate(col_order)
    }
    betas = plane_sum(sums[0], sums[X], sums[Y], sums[X | Y], swap_col, halves)

    trail_cols, keep, send = tail(
        alphas,
        betas,
        trail_lbar,
        trail_factor,
        heads,
        head_lbar.reshape(6, step, NB),
        place,
        rels,
    )
    total = (keep + swap_col(send, CORE)).reshape(4, rows, 6, step, NB)
    parts = plane_sum(total[0], total[1], total[2], total[3], swap_col, halves)
    total = parts[0] + parts[1] + parts[2]
    head_adj = total[0] + swap_row(total[1], 2) + swap_row(total[2], 1) + swap_row(total[3], 3)
    return trail_cols, head_adj.reshape(6, step * NB)


def body(*operands):
    rows, cols = lax.axis_size("row"), lax.axis_size("col")
    m = operands[1].shape[0]
    if rows == 4 and cols == 8 and m % 128 == 0:
        return fast_body(*operands)
    return general_body(*operands)


def solution(mesh):
    in_specs = (
        P(None, "col", "row"),
        P(("row", "col"), None),
        P(("row", "col"), None),
        P(None, ("row", "col")),
        P(None, ("row", "col")),
        P(None, ("row", "col")),
    )
    out_specs = (P(("row", "col"), None), P(None, ("row", "col")))
    return jax.shard_map(body, mesh=mesh, in_specs=in_specs, out_specs=out_specs, check_vma=False)
```
